32 devices in a mesh: gx: 8 (over z, y), gy: 4 (over x, core).
Axes of the slice: x: 2, y: 2, z: 4, core: 2. Of those that a mesh axis runs over, the one named last changes fastest.
Arguments:
- coarse_send: bfloat16 [8, 35, 4096], P('gx', None, 'gy'), may hold values from -6 to 6
- coarse_flux: float32 [8, 35, 1024], P('gx', None, 'gy'), may hold values from -6 to 6
- patch_owner: int32 [8], replicated, may hold values from 0 to 15, as said below
- velocity: float32 [3], replicated, may hold values from -0.6 to 0.6
- diffusivity: float32 [35], replicated, may hold values from 0.03 to 0.15
- stoich: float32 [35, 35], replicated, may hold values from -1 to 1
Outputs:
- fine_state: float32 [16, 35, 32768], P('gx', None, 'gy')
- reflux: float32 [8, 35, 1024], P('gx', None, 'gy')
The draws below stay inside these ranges and needn't reach their ends.
Inputs may be any that keep to these rules, and one draw needn't show every extreme that they name: `patch_owner`: the 8 entries are distinct; slot s belongs to owner group s // 2, the group of index s // 2 along gx; a group owns 0, 1 or 2 patches, and at least one group owns exactly 2.
All inputs are finite; a program needn't handle non-finite values.
Results may differ from the reference program's by a relative error of at most 0.0003.
Values may be sent and summed in bfloat16 or wider, within the bound.
No kernel may reach another device: no remote copies, remote signals or barrier semaphores. Data moves between devices by JAX's collectives and lax.ppermute only.
A program may use at most 128 MiB of HBM per device.

```python
import math
import jax
import jax.numpy as jnp
from jax import lax

FIELDS = 35
CB = 16
SEND = 1
OWN = 2
NP = 8
NO = 16


def draw_patch_owner(key, part):
    key_perm, key_bits = jax.random.split(jax.random.fold_in(key, 17), 2)
    groups_total = NP // SEND
    half_way = groups_total // 2
    partner = jax.random.permutation(key_perm, groups_total).astype(jnp.int32)
    first_value = partner[0]
    partner = jnp.where(partner == half_way, first_value, partner).astype(jnp.int32)
    partner = partner.at[0].set(half_way).astype(jnp.int32)
    moved = jax.random.randint(key_bits, (NP,), 0, 2).astype(jnp.int32)
    patch_index = jnp.arange(NP, dtype=jnp.int32)
    source_group = (patch_index // SEND).astype(jnp.int32)
    within = (patch_index % SEND).astype(jnp.int32)
    moved = jnp.where(source_group == 0, 1, jnp.where(source_group == half_way, 0, moved)).astype(jnp.int32)
    target = jnp.where(moved == 1, partner[source_group], source_group).astype(jnp.int32)
    return (target * OWN + moved * SEND + within).astype(jnp.int32)


def block_scale(rng, dims, cuts, smallest, top_value):
    gain = 1.0
    for dim, shards_of in cuts:
        heights = jax.random.uniform(jax.random.fold_in(jax.random.fold_in(rng, 6), dim), (shards_of,), jnp.float32, smallest / len(cuts), top_value / len(cuts))
        gain = gain * jnp.repeat(jnp.exp(heights), dims[dim] // shards_of).reshape((-1,) + (1,) * (len(dims) - 1 - dim))
    return gain


def bell_draw(rng, shape, width, bound, shards=(), kind=jnp.bfloat16):
    gain = block_scale(rng, shape, shards, -0.22, 0.18) if shards else 1.0
    drawn = jax.random.normal(rng, shape, jnp.float32) * width * gain
    return jnp.minimum(jnp.maximum(drawn, -bound), bound).astype(kind)


def setup_inputs(seed: int = 0) -> dict:
    splits = jax.random.split(jax.random.key(seed), 7)
    coarse_send = bell_draw(splits[0], (NP, FIELDS, CB * CB * CB), 1.0, 6.0, ((0, 8), (2, 4)))
    coarse_flux = bell_draw(splits[1], (NP, FIELDS, CB * 4 * CB), 1.0, 6.0, ((0, 8), (2, 4)), jnp.float32)
    patch_owner = draw_patch_owner(jax.random.fold_in(splits[6], 71), 0)
    velocity = jnp.clip(jax.random.uniform(splits[3], (3,), jnp.float32, -0.6, 0.6), -0.6, 0.6)
    diffusivity = jnp.clip(jnp.exp(jax.random.uniform(splits[4], (FIELDS,), jnp.float32, math.log(0.03), math.log(0.15))), 0.03, 0.15)
    stoich = bell_draw(splits[5], (FIELDS, FIELDS), FIELDS ** -0.5, 1.0, (), jnp.float32)
    return dict(coarse_send=coarse_send, coarse_flux=coarse_flux, patch_owner=patch_owner, velocity=velocity, diffusivity=diffusivity, stoich=stoich)


time_step = 0.25
heat_gain = 2.0
highest = lax.Precision.HIGHEST


def axis_slope(values, axis):
    moved = jnp.moveaxis(values, axis, 0)
    middle = (moved[2:] - moved[:-2]) * 0.5
    joined = jnp.concatenate([moved[1:2] - moved[0:1], middle, moved[-1:] - moved[-2:-1]], 0)
    return jnp.moveaxis(joined, 0, axis)


def spread(values):
    return values[..., :, None, :, None, :, None]


def refine(coarse, slope_z, slope_y, slope_x):
    offsets = jnp.array([-0.5, 0.5], jnp.float32)
    leading = coarse.shape[:-3]
    depth, height, breadth = coarse.shape[-3:]
    shift_y = offsets[:, None, None]
    shift_z = offsets[:, None, None, None, None]
    terms = spread(slope_x) * offsets + spread(slope_y) * shift_y + spread(slope_z) * shift_z
    fine_cells = spread(coarse) + terms * 0.5
    return fine_cells.reshape(leading + (2 * depth, 2 * height, 2 * breadth))


def face_flux(left_side, right_side, speed, diffuse):
    return speed * (left_side + right_side) * 0.5 - diffuse * (right_side - left_side)


def tendency(padded_layers, cells, velocity, diffusivity, stoich):
    diffuse = diffusivity[:, None, None, None]
    padded_cols = jnp.concatenate([cells[..., :1], cells, cells[..., -1:]], -1)
    padded_rows = jnp.concatenate([cells[..., :1, :], cells, cells[..., -1:, :]], -2)
    flux_cols = face_flux(padded_cols[..., :-1], padded_cols[..., 1:], velocity[0], diffuse)
    flux_rows = face_flux(padded_rows[..., :-1, :], padded_rows[..., 1:, :], velocity[1], diffuse)
    flux_layers = face_flux(padded_layers[..., :-1, :, :], padded_layers[..., 1:, :, :], velocity[2], diffuse)
    outflow = (flux_cols[..., 1:] - flux_cols[..., :-1]) + (flux_rows[..., 1:, :] - flux_rows[..., :-1, :]) + (flux_layers[..., 1:, :, :] - flux_layers[..., :-1, :, :])
    reaction_rate = cells * jax.nn.sigmoid(heat_gain * cells[..., 0:1, :, :, :])
    source = jnp.einsum('fg,...gzyx->...fzyx', stoich, reaction_rate, precision=highest)
    side_fluxes = (flux_cols[..., 0], flux_cols[..., -1], flux_rows[..., 0, :], flux_rows[..., -1, :])
    return source - outflow, side_fluxes


def average_sides(earlier, later_sides):
    return jnp.stack([(earlier[0] + later_sides[0]) * 0.5, (earlier[1] + later_sides[1]) * 0.5, (earlier[2] + later_sides[2]) * 0.5, (earlier[3] + later_sides[3]) * 0.5], -2)


def coarsen_faces(register):
    leading = register.shape[:-3]
    depth = register.shape[-3] // 2
    along = register.shape[-1] // 2
    split_faces = register.reshape(leading + (depth, 2, 4, along, 2))
    return (split_faces[..., 0, :, :, 0] + split_faces[..., 0, :, :, 1] + split_faces[..., 1, :, :, 0] + split_faces[..., 1, :, :, 1]) * 0.25


def extend_edge(cells):
    return jnp.concatenate([cells[..., :1, :, :], cells, cells[..., -1:, :, :]], -3)


def reference(coarse_send, coarse_flux, patch_owner, velocity, diffusivity, stoich):
    def one_patch(inputs):
        coarse_block, face_values = inputs
        coarse = coarse_block.astype(jnp.float32).reshape(FIELDS, CB, CB, CB)
        fine_cells = refine(coarse, axis_slope(coarse, 1), axis_slope(coarse, 2), axis_slope(coarse, 3))
        change, first_sides = tendency(extend_edge(fine_cells), fine_cells, velocity, diffusivity, stoich)
        section_state = fine_cells + time_step * change
        second, second_sides = tendency(extend_edge(section_state), section_state, velocity, diffusivity, stoich)
        final_state = fine_cells + (time_step * 0.5) * (change + second)
        register = average_sides(first_sides, second_sides)
        corrected = coarsen_faces(register) - face_values.reshape(FIELDS, CB, 4, CB)
        return final_state.reshape(FIELDS, -1), corrected.reshape(FIELDS, -1)

    fine_all, reflux = lax.map(one_patch, (coarse_send, coarse_flux))
    fine_state = jnp.zeros((NO,) + fine_all.shape[1:], jnp.float32).at[patch_owner].set(fine_all)
    return fine_state, reflux
```

```python
import functools

import jax
import jax.numpy as jnp
import numpy as np
from jax import lax
from jax.experimental import pallas as pl
from jax.experimental.pallas import tpu as pltpu
from jax.sharding import PartitionSpec as P

CB = 16
FINE = 2 * CB
CELLS = CB * CB
AREA = FINE * FINE
TILE = 128
ROWS = 40
PAD = 48
DIRECT = 8

time_step = 0.25
heat_gain = 2.0


def interpolation():
    slope = np.zeros((CB, CB), np.float32)
    for i in range(1, CB - 1):
        slope[i + 1, i], slope[i - 1, i] = 0.5, -0.5
    slope[1, 0], slope[0, 0] = 1.0, -1.0
    slope[-1, -1], slope[-2, -1] = 1.0, -1.0
    copy = np.zeros((CB, FINE), np.float32)
    tilt = np.zeros((CB, FINE), np.float32)
    for i in range(CB):
        for a in range(2):
            copy[i, 2 * i + a] = 1.0
            tilt[:, 2 * i + a] = slope[:, i] * (a - 0.5) * 0.5
    same = np.kron(copy, copy)
    full = same + np.kron(copy, tilt) + np.kron(tilt, copy)
    return full, same


def strips():
    edge = np.arange(FINE)
    last = FINE - 1
    border = [edge * FINE, edge * FINE + last, edge, last * FINE + edge]
    inner = [edge * FINE + 1, edge * FINE + last - 1, FINE + edge, (last - 1) * FINE + edge]
    return np.concatenate(border), np.concatenate(inner)


def pair_sums(layers):
    place = np.zeros((layers * TILE, layers * TILE // 2), np.float32)
    for k in range(layers):
        for lane in range(TILE):
            place[k * TILE + lane, k * TILE // 2 + lane // 2] = 0.25
    return place


def fill_coarse(stack, own, low, high, layers):
    fields = own.shape[1]
    stack[...] = jnp.zeros_like(stack)
    for k in range(layers + 4):
        if k < 2:
            source, at = low, k
        elif k < layers + 2:
            source, at = own, k - 2
        else:
            source, at = high, k - layers - 2
        stack[k * PAD : k * PAD + fields, :] = source[0, :, at * CELLS : (at + 1) * CELLS]


def edge_ghosts(parts, bottom, top, layers, width):
    def rows(k):
        return slice((k + 2) * PAD, (k + 2) * PAD + ROWS)

    @pl.when(bottom)
    def _():
        parts[rows(-1), width:] = 2.0 * parts[rows(0), width:] - parts[rows(1), width:]

    @pl.when(top)
    def _():
        parts[rows(layers), width:] = (
            2.0 * parts[rows(layers - 1), width:] - parts[rows(layers - 2), width:]
        )


def fine_layers(start, parts, layers, width):
    step = 2 * TILE

    def rows(k):
        return pl.ds(pl.multiple_of((k + 1) * PAD, 16), ROWS)

    def body(k, carry):
        for c in range(0, width, step):
            lanes = slice(c, c + step)
            copies = slice(width + c, width + c + step)
            centre = parts[rows(k), lanes]
            tilt = (parts[rows(k + 1), copies] - parts[rows(k - 1), copies]) * 0.125
            start[2 * k, :, lanes] = centre - tilt
            start[2 * k + 1, :, lanes] = centre + tilt
        return carry

    lax.fori_loop(0, layers + 2, body, 0)


def split_coupling(coupling):
    value = coupling[...]
    head = value.astype(jnp.bfloat16)
    rest = (value - head.astype(jnp.float32)).astype(jnp.bfloat16)
    column = lax.broadcasted_iota(jnp.int32, value.shape, 1)
    return jnp.where(column < 2 * PAD, head.astype(jnp.float32), rest.astype(jnp.float32)).astype(
        jnp.bfloat16
    )


def store_rate(rate, lanes, cells, warm):
    value = cells * warm
    head = value.astype(jnp.bfloat16)
    rest = (value - head.astype(jnp.float32)).astype(jnp.bfloat16)
    rate[0:ROWS, lanes] = head
    rate[PAD : PAD + ROWS, lanes] = rest
    rate[2 * PAD : 2 * PAD + ROWS, lanes] = head


def sources(rate, mixed):
    return jnp.dot(mixed, rate[...], preferred_element_type=jnp.float32)


def stage(field, z, rate, mixed, velocity, diffuse, emit):
    count = AREA // TILE
    lane = lax.broadcasted_iota(jnp.int32, (ROWS, TILE), 1)
    pos = lane % FINE
    at_low, at_high = pos == 0, pos == FINE - 1
    head, tail = lane < FINE, lane >= TILE - FINE
    half = [velocity[d] * 0.5 for d in range(3)]
    warm = jax.nn.sigmoid(heat_gain * field[z, 0:1, :])
    for t in range(count):
        lanes = slice(t * TILE, (t + 1) * TILE)
        store_rate(rate, lanes, field[z, :, lanes], warm[:, lanes])
    source = sources(rate, mixed)
    tiles = {}
    ups = {}
    downs = {}

    def tile(t):
        if t not in tiles:
            tiles[t] = field[z, :, t * TILE : (t + 1) * TILE]
            ups[t] = pltpu.roll(tiles[t], TILE - FINE, 1)
            downs[t] = pltpu.roll(tiles[t], FINE, 1)
        return tiles[t]

    for t in range(count):
        lanes = slice(t * TILE, (t + 1) * TILE)
        cells = tile(t)
        x_low = jnp.where(at_low, cells, pltpu.roll(cells, 1, 1))
        x_high = jnp.where(at_high, cells, pltpu.roll(cells, TILE - 1, 1))
        if t + 1 < count:
            tile(t + 1)
        y_low = jnp.where(head, downs[t - 1] if t else cells, downs[t])
        y_high = jnp.where(tail, ups[t + 1] if t + 1 < count else cells, ups[t])
        z_low = field[z - 1, :, lanes]
        z_high = field[z + 1, :, lanes]
        drift = (
            half[0] * (x_high - x_low) + half[1] * (y_high - y_low) + half[2] * (z_high - z_low)
        )
        spread = (x_high + x_low) + (y_high + y_low) + (z_high + z_low) - 6.0 * cells
        emit(lanes, cells, source[:, lanes] - drift + diffuse * spread)


def step_kernel(
    layers,
    flags,
    velocity,
    own,
    low,
    high,
    weights,
    coupling,
    diffusivity,
    out,
    stack,
    parts,
    start,
    middle,
    rate,
):
    bottom, top = flags[0] == 1, flags[1] == 1
    fields = own.shape[1]
    depth = 2 * layers
    rate[...] = jnp.zeros_like(rate)
    fill_coarse(stack, own, low, high, layers)
    parts[...] = jnp.dot(stack[...], weights[...], preferred_element_type=jnp.float32)
    edge_ghosts(parts, bottom, top, layers, AREA)
    fine_layers(start, parts, layers, AREA)

    @pl.when(bottom)
    def _():
        start[1] = start[2]

    @pl.when(top)
    def _():
        start[depth + 2] = start[depth + 1]

    mixed = split_coupling(coupling)
    diffuse = jnp.broadcast_to(diffusivity[...], (ROWS, TILE))

    def first(i, carry):
        def emit(lanes, cells, change):
            middle[i, :, lanes] = cells + time_step * change

        stage(start, i + 1, rate, mixed, velocity, diffuse, emit)
        return carry

    lax.fori_loop(0, depth + 2, first, 0)

    @pl.when(bottom)
    def _():
        middle[0] = middle[1]

    @pl.when(top)
    def _():
        middle[depth + 1] = middle[depth]

    def second(i, carry):
        def emit(lanes, cells, change):
            value = (start[i + 2, :, lanes] + cells) * 0.5 + (time_step * 0.5) * change
            at = pl.multiple_of(i * AREA + lanes.start, TILE)
            out[0, :, pl.ds(at, TILE)] = value[:fields]

        stage(middle, i + 1, rate, mixed, velocity, diffuse, emit)
        return carry

    lax.fori_loop(0, depth, second, 0)


def side_kernel(
    layers,
    flags,
    velocity,
    own,
    low,
    high,
    weights,
    coupling,
    diffusivity,
    place,
    fluxes,
    out,
    stack,
    parts,
    start,
    rate,
    faces,
):
    bottom, top = flags[0] == 1, flags[1] == 1
    fields = own.shape[1]
    depth = 2 * layers
    width = 2 * TILE
    rate[...] = jnp.zeros_like(rate)
    fill_coarse(stack, own, low, high, layers)
    parts[...] = jnp.dot(stack[...], weights[...], preferred_element_type=jnp.float32)
    edge_ghosts(parts, bottom, top, layers, width)
    fine_layers(start, parts, layers, width)

    @pl.when(bottom)
    def _():
        start[1] = start[2]

    @pl.when(top)
    def _():
        start[depth + 2] = start[depth + 1]

    mixed = split_coupling(coupling)
    diffuse = jnp.broadcast_to(diffusivity[...], (ROWS, TILE))
    lane = lax.broadcasted_iota(jnp.int32, (ROWS, TILE), 1)
    pos = lane % FINE
    side = lane // FINE
    at_low, at_high = pos == 0, pos == FINE - 1
    normal = jnp.where(side < 2, velocity[0], velocity[1])
    along = jnp.where(side < 2, velocity[1], velocity[0]) * 0.5
    inward = jnp.where(side % 2 == 0, normal, -normal) * 0.5
    half_z = velocity[2] * 0.5
    border = slice(0, TILE)
    inner = slice(TILE, 2 * TILE)
    for i in range(depth):
        warm = jax.nn.sigmoid(heat_gain * start[i + 2, 0:1, border])
        store_rate(rate, slice(i * TILE, (i + 1) * TILE), start[i + 2, :, border], warm)
    source = sources(rate, mixed)
    totals = []
    for i in range(depth):
        cells = start[i + 2, :, border]
        gap = start[i + 2, :, inner] - cells
        behind = jnp.where(at_low, cells, pltpu.roll(cells, 1, 1))
        ahead = jnp.where(at_high, cells, pltpu.roll(cells, TILE - 1, 1))
        z_low = start[i + 1, :, border]
        z_high = start[i + 3, :, border]
        drift = inward * gap + along * (ahead - behind) + half_z * (z_high - z_low)
        spread = gap + (ahead + behind) + (z_high + z_low) - 4.0 * cells
        change = source[:, i * TILE : (i + 1) * TILE] - drift + diffuse * spread
        later = cells + time_step * change
        totals.append((normal * cells + normal * later) * 0.5)
    for k in range(layers):
        faces[:, k * TILE : (k + 1) * TILE] = totals[2 * k] + totals[2 * k + 1]
    summed = jnp.dot(
        faces[...],
        place[...],
        precision=lax.Precision.HIGHEST,
        preferred_element_type=jnp.float32,
    )
    out[0] = summed[:fields] - fluxes[0]


def whole(shape):
    return pl.BlockSpec(shape, lambda s: (0,) * len(shape))


def per_slot(shape):
    return pl.BlockSpec((1,) + shape, lambda s: (s,) + (0,) * len(shape))


def scalars():
    return pl.BlockSpec(memory_space=pltpu.SMEM)


def fine_step(flags, velocity, own, low, high, coupling, diffusivity):
    slots, fields, cells = own.shape
    layers = cells // CELLS
    full, same = interpolation()
    weights = jnp.asarray(np.concatenate([full, same], 1), jnp.bfloat16)
    return pl.pallas_call(
        functools.partial(step_kernel, layers),
        grid=(slots,),
        in_specs=[
            scalars(),
            scalars(),
            per_slot((fields, cells)),
            per_slot((fields, 2 * CELLS)),
            per_slot((fields, 2 * CELLS)),
            whole(weights.shape),
            whole(coupling.shape),
            whole(diffusivity.shape),
        ],
        out_specs=per_slot((fields, 2 * layers * AREA)),
        out_shape=jax.ShapeDtypeStruct((slots, fields, 2 * layers * AREA), jnp.float32),
        scratch_shapes=[
            pltpu.VMEM(((layers + 4) * PAD, CELLS), jnp.bfloat16),
            pltpu.VMEM(((layers + 4) * PAD, 2 * AREA), jnp.float32),
            pltpu.VMEM((2 * layers + 4, ROWS, AREA), jnp.float32),
            pltpu.VMEM((2 * layers + 2, ROWS, AREA), jnp.float32),
            pltpu.VMEM((3 * PAD, AREA), jnp.bfloat16),
        ],
        cost_estimate=pl.CostEstimate(
            flops=slots * 2000000000, bytes_accessed=8000000, transcendentals=0
        ),
        name="fine_step",
    )(flags, velocity, own, low, high, weights, coupling, diffusivity)


def side_fluxes(flags, velocity, own, low, high, coupling, diffusivity, fluxes):
    slots, fields, cells = own.shape
    layers = cells // CELLS
    full, same = interpolation()
    border, inner = strips()
    picked = np.concatenate([border, inner])
    weights = jnp.asarray(np.concatenate([full[:, picked], same[:, picked]], 1), jnp.bfloat16)
    place = jnp.asarray(pair_sums(layers))
    return pl.pallas_call(
        functools.partial(side_kernel, layers),
        grid=(slots,),
        in_specs=[
            scalars(),
            scalars(),
            per_slot((fields, cells)),
            per_slot((fields, 2 * CELLS)),
            per_slot((fields, 2 * CELLS)),
            whole(weights.shape),
            whole(coupling.shape),
            whole(diffusivity.shape),
            whole(place.shape),
            per_slot(fluxes.shape[1:]),
        ],
        out_specs=per_slot(fluxes.shape[1:]),
        out_shape=jax.ShapeDtypeStruct(fluxes.shape, jnp.float32),
        scratch_shapes=[
            pltpu.VMEM(((layers + 4) * PAD, CELLS), jnp.bfloat16),
            pltpu.VMEM(((layers + 4) * PAD, 4 * TILE), jnp.float32),
            pltpu.VMEM((2 * layers + 4, ROWS, 2 * TILE), jnp.float32),
            pltpu.VMEM((3 * PAD, 2 * layers * TILE), jnp.bfloat16),
            pltpu.VMEM((ROWS, layers * TILE), jnp.float32),
        ],
        cost_estimate=pl.CostEstimate(
            flops=slots * 400000000, bytes_accessed=2000000, transcendentals=0
        ),
        name="side_fluxes",
    )(flags, velocity, own, low, high, weights, coupling, diffusivity, place, fluxes)


def halo(block):
    count = lax.axis_size("gy")
    forward = [(i, i + 1) for i in range(count - 1)]
    backward = [(i + 1, i) for i in range(count - 1)]
    low = lax.ppermute(block[:, :, -2 * CELLS :], "gy", forward)
    high = lax.ppermute(block[:, :, : 2 * CELLS], "gy", backward)
    return low, high


def fetch(coarse, patch_owner, my_slots):
    groups = lax.axis_size("gx")
    group = lax.axis_index("gx")
    send_slots = coarse.shape[0]
    if groups > DIRECT:
        chooser = (my_slots[:, None] == patch_owner[None, :]).astype(coarse.dtype)
        everything = lax.all_gather(coarse, "gx", axis=0, tiled=True)
        return jnp.einsum("oq,qfc->ofc", chooser, everything)
    blocks = [coarse] + [
        lax.ppermute(coarse, "gx", [(i, (i + shift) % groups) for i in range(groups)])
        for shift in range(1, groups)
    ]
    picked = []
    for s in range(my_slots.shape[0]):
        value = jnp.zeros_like(coarse[0])
        for shift in range(groups):
            origin = lax.rem(group - shift + groups, groups)
            for t in range(send_slots):
                owner = lax.dynamic_index_in_dim(
                    patch_owner, origin * send_slots + t, 0, keepdims=False
                )
                value = jnp.where(owner == my_slots[s], blocks[shift][t], value)
        picked.append(value)
    return jnp.stack(picked)


def shards(coarse_send, coarse_flux, patch_owner, velocity, diffusivity, stoich):
    send_slots, fields, _ = coarse_send.shape
    own_slots = 2 * send_slots
    pencil = lax.axis_index("gy")
    pencils = lax.axis_size("gy")
    my_slots = lax.axis_index("gx") * own_slots + jnp.arange(own_slots, dtype=jnp.int32)
    flags = jnp.stack([pencil == 0, pencil == pencils - 1]).astype(jnp.int32)
    square = jnp.pad(stoich, ((0, ROWS - fields), (0, PAD - fields)))
    coupling = jnp.concatenate([square, square, square], 1)
    diffuse = jnp.pad(diffusivity, (0, ROWS - fields)).reshape(ROWS, 1)
    low, high = halo(coarse_send)
    coarse = fetch(coarse_send, patch_owner, my_slots)
    reflux = side_fluxes(
        flags, velocity, coarse_send, low, high, coupling, diffuse, coarse_flux
    )
    slot_low, slot_high = halo(coarse)
    fine_state = fine_step(
        flags, velocity, coarse, slot_low, slot_high, coupling, diffuse
    )
    return fine_state, reflux


def solution(mesh):
    placed = (P("gx", None, "gy"), P("gx", None, "gy"), P(), P(), P(), P())
    return jax.shard_map(
        shards,
        mesh=mesh,
        in_specs=placed,
        out_specs=(P("gx", None, "gy"), P("gx", None, "gy")),
        check_vma=False,
    )
```

```python
import functools

import jax
import jax.numpy as jnp
import numpy as np
from jax import lax
from jax.experimental import pallas as pl
from jax.experimental.pallas import tpu as pltpu
from jax.sharding import PartitionSpec as P

CB = 16
FINE = 2 * CB
CELLS = CB * CB
AREA = FINE * FINE
TILE = 128
DIRECT = 8

time_step = 0.25
heat_gain = 2.0


def interpolation():
    slope = np.zeros((CB, CB), np.float32)
    for i in range(1, CB - 1):
        slope[i + 1, i], slope[i - 1, i] = 0.5, -0.5
    slope[1, 0], slope[0, 0] = 1.0, -1.0
    slope[-1, -1], slope[-2, -1] = 1.0, -1.0
    copy = np.zeros((CB, FINE), np.float32)
    tilt = np.zeros((CB, FINE), np.float32)
    for i in range(CB):
        for a in range(2):
            copy[i, 2 * i + a] = 1.0
            tilt[:, 2 * i + a] = slope[:, i] * (a - 0.5) * 0.5
    same = np.kron(copy, copy)
    full = same + np.kron(copy, tilt) + np.kron(tilt, copy)
    return full, same


def strips():
    edge = np.arange(FINE)
    last = FINE - 1
    border = [edge * FINE, edge * FINE + last, edge, last * FINE + edge]
    inner = [edge * FINE + 1, edge * FINE + last - 1, FINE + edge, (last - 1) * FINE + edge]
    return np.concatenate(border), np.concatenate(inner)


def pair_sums(layers):
    place = np.zeros((layers * TILE, layers * TILE // 2), np.float32)
    for k in range(layers):
        for lane in range(TILE):
            place[k * TILE + lane, k * TILE // 2 + lane // 2] = 0.25
    return place


def up(value, unit):
    return -(-value // unit) * unit


def equal(shape, left, right):
    rows = lax.broadcasted_iota(jnp.int32, shape, 0)
    columns = lax.broadcasted_iota(jnp.int32, shape, 1)
    return left(rows) == right(columns)


def fill_coarse(stack, blocks, rows, layers):
    slots = len(blocks)
    fields = blocks[0].shape[0]
    mixed = None
    for s in range(slots):
        spot = equal((rows, fields), lambda r: r, lambda f: f * slots + s)
        part = jnp.dot(
            spot.astype(jnp.float32).astype(jnp.bfloat16),
            blocks[s],
            preferred_element_type=jnp.float32,
        )
        mixed = part if mixed is None else mixed + part
    pad = up(rows, 16)
    for k in range(layers + 4):
        stack[k * pad : k * pad + rows, :] = mixed[:, k * CELLS : (k + 1) * CELLS].astype(
            jnp.bfloat16
        )


def edge_ghosts(parts, bottom, top, layers, width, count):
    pad = up(count, 16)

    def rows(k):
        return slice((k + 2) * pad, (k + 2) * pad + count)

    @pl.when(bottom)
    def _():
        parts[rows(-1), width:] = 2.0 * parts[rows(0), width:] - parts[rows(1), width:]

    @pl.when(top)
    def _():
        parts[rows(layers), width:] = (
            2.0 * parts[rows(layers - 1), width:] - parts[rows(layers - 2), width:]
        )


def fine_layers(start, parts, layers, width, count):
    step = 2 * TILE
    pad = up(count, 16)

    def rows(k):
        return pl.ds(pl.multiple_of((k + 1) * pad, 16), count)

    def body(k, carry):
        for c in range(0, width, step):
            lanes = slice(c, c + step)
            copies = slice(width + c, width + c + step)
            centre = parts[rows(k), lanes]
            tilt = (parts[rows(k + 1), copies] - parts[rows(k - 1), copies]) * 0.125
            start[2 * k, :, lanes] = centre - tilt
            start[2 * k + 1, :, lanes] = centre + tilt
        return carry

    lax.fori_loop(0, layers + 2, body, 0)


def exact_dot(left, right):
    return jnp.dot(
        left, right, precision=lax.Precision.HIGHEST, preferred_element_type=jnp.float32
    )


def split_coupling(stoich, slots, rows):
    value = stoich[...]
    fields = value.shape[0]
    pad = up(rows, 16)
    width = 3 * pad
    rise = equal((rows, fields), lambda r: r // slots, lambda f: f).astype(jnp.float32)
    run = equal((fields, width), lambda f: f, lambda c: c % pad // slots).astype(jnp.float32)
    spread = exact_dot(rise, exact_dot(value, run))
    shape = (rows, width)
    spread = jnp.where(equal(shape, lambda r: r % slots, lambda c: c % pad % slots), spread, 0.0)
    head = spread.astype(jnp.bfloat16)
    rest = (spread - head.astype(jnp.float32)).astype(jnp.bfloat16)
    column = lax.broadcasted_iota(jnp.int32, shape, 1)
    return jnp.where(
        column < 2 * pad, head.astype(jnp.float32), rest.astype(jnp.float32)
    ).astype(jnp.bfloat16)


def spread_diffusivity(diffusivity, slots, rows):
    field = lax.broadcasted_iota(jnp.int32, (rows, TILE), 0) // slots
    value = jnp.zeros((rows, TILE), jnp.float32)
    for f in range(diffusivity.shape[0]):
        value = jnp.where(field == f, diffusivity[f], value)
    return value


def warmth(field, slots):
    warm = jax.nn.sigmoid(heat_gain * field[0:slots])
    row = lax.broadcasted_iota(jnp.int32, (8, field.shape[1]), 0) % slots
    value = jnp.broadcast_to(warm[0:1], row.shape)
    for s in range(1, slots):
        value = jnp.where(row == s, warm[s : s + 1], value)
    return value


def store_rate(rate, lanes, cells, warm):
    rows = cells.shape[0]
    pad = up(rows, 16)
    value = cells * jnp.concatenate([warm] * (rows // 8), 0)
    head = value.astype(jnp.bfloat16)
    rest = (value - head.astype(jnp.float32)).astype(jnp.bfloat16)
    rate[0:rows, lanes] = head
    rate[pad : pad + rows, lanes] = rest
    rate[2 * pad : 2 * pad + rows, lanes] = head


def sources(rate, mixed):
    return jnp.dot(mixed, rate[...], preferred_element_type=jnp.float32)


def stage(field, z, slots, rate, mixed, velocity, diffuse, emit):
    count = AREA // TILE
    lane = lax.broadcasted_iota(jnp.int32, diffuse.shape, 1)
    pos = lane % FINE
    at_low, at_high = pos == 0, pos == FINE - 1
    head, tail = lane < FINE, lane >= TILE - FINE
    half = [velocity[d] * 0.5 for d in range(3)]
    warm = warmth(field[z, 0:8, :], slots)
    for t in range(count):
        lanes = slice(t * TILE, (t + 1) * TILE)
        store_rate(rate, lanes, field[z, :, lanes], warm[:, lanes])
    source = sources(rate, mixed)
    tiles = {}
    ups = {}
    downs = {}

    def tile(t):
        if t not in tiles:
            tiles[t] = field[z, :, t * TILE : (t + 1) * TILE]
            ups[t] = pltpu.roll(tiles[t], TILE - FINE, 1)
            downs[t] = pltpu.roll(tiles[t], FINE, 1)
        return tiles[t]

    for t in range(count):
        lanes = slice(t * TILE, (t + 1) * TILE)
        cells = tile(t)
        x_low = jnp.where(at_low, cells, pltpu.roll(cells, 1, 1))
        x_high = jnp.where(at_high, cells, pltpu.roll(cells, TILE - 1, 1))
        if t + 1 < count:
            tile(t + 1)
        y_low = jnp.where(head, downs[t - 1] if t else cells, downs[t])
        y_high = jnp.where(tail, ups[t + 1] if t + 1 < count else cells, ups[t])
        z_low = field[z - 1, :, lanes]
        z_high = field[z + 1, :, lanes]
        drift = (
            half[0] * (x_high - x_low) + half[1] * (y_high - y_low) + half[2] * (z_high - z_low)
        )
        spread = (x_high + x_low) + (y_high + y_low) + (z_high + z_low) - 6.0 * cells
        emit(lanes, cells, source[:, lanes] - drift + diffuse * spread)


def step_kernel(layers, slots, direct, velocity, owner, stoich, diffusivity, weights, *refs):
    blocks = refs[:-7]
    out, picked, stack, parts, start, middle, rate = refs[-7:]
    pencil = lax.axis_index("gy")
    bottom, top = pencil == 0, pencil == lax.axis_size("gy") - 1
    depth = 2 * layers
    rows = start.shape[1]
    rate[...] = jnp.zeros_like(rate)
    if direct:
        groups = lax.axis_size("gx")
        group = lax.axis_index("gx")
        picked[...] = jnp.zeros_like(picked)
        for j, block in enumerate(blocks):
            origin = lax.rem(group - j + groups, groups)
            for t in range(block.shape[0]):
                slot = owner[origin * block.shape[0] + t] - group * slots
                for s in range(slots):

                    @pl.when(slot == s)
                    def _():
                        picked[s] = block[t]
    else:
        picked[...] = blocks[0][...]
    fill_coarse(stack, [picked[s] for s in range(slots)], rows, layers)
    parts[...] = jnp.dot(stack[...], weights[...], preferred_element_type=jnp.float32)
    edge_ghosts(parts, bottom, top, layers, AREA, rows)
    fine_layers(start, parts, layers, AREA, rows)

    @pl.when(bottom)
    def _():
        start[1] = start[2]

    @pl.when(top)
    def _():
        start[depth + 2] = start[depth + 1]

    mixed = split_coupling(stoich, slots, rows)
    diffuse = spread_diffusivity(diffusivity, slots, rows)

    def first(i, carry):
        def emit(lanes, cells, change):
            middle[i, :, lanes] = cells + time_step * change

        stage(start, i + 1, slots, rate, mixed, velocity, diffuse, emit)
        return carry

    lax.fori_loop(0, depth + 2, first, 0)

    @pl.when(bottom)
    def _():
        middle[0] = middle[1]

    @pl.when(top)
    def _():
        middle[depth + 1] = middle[depth]

    def second(i, carry):
        def emit(lanes, cells, change):
            value = (start[i + 2, :, lanes] + cells) * 0.5 + (time_step * 0.5) * change
            at = pl.multiple_of(i * AREA + lanes.start, TILE)
            for f in range(out.shape[0]):
                out[f, :, pl.ds(at, TILE)] = value[f * slots : (f + 1) * slots]

        stage(middle, i + 1, slots, rate, mixed, velocity, diffuse, emit)
        return carry

    lax.fori_loop(0, depth, second, 0)


def side_kernel(
    layers, velocity, stoich, diffusivity, weights, place, fluxes, block, out, stack, parts,
    start, rate, faces,
):
    pencil = lax.axis_index("gy")
    bottom, top = pencil == 0, pencil == lax.axis_size("gy") - 1
    fields = block.shape[1]
    depth = 2 * layers
    width = 2 * TILE
    rows = start.shape[1]
    rate[...] = jnp.zeros_like(rate)
    fill_coarse(stack, [block[0]], rows, layers)
    parts[...] = jnp.dot(stack[...], weights[...], preferred_element_type=jnp.float32)
    edge_ghosts(parts, bottom, top, layers, width, rows)
    fine_layers(start, parts, layers, width, rows)

    @pl.when(bottom)
    def _():
        start[1] = start[2]

    @pl.when(top)
    def _():
        start[depth + 2] = start[depth + 1]

    mixed = split_coupling(stoich, 1, rows)
    diffuse = spread_diffusivity(diffusivity, 1, rows)
    lane = lax.broadcasted_iota(jnp.int32, (rows, TILE), 1)
    pos = lane % FINE
    side = lane // FINE
    at_low, at_high = pos == 0, pos == FINE - 1
    normal = jnp.where(side < 2, velocity[0], velocity[1])
    along = jnp.where(side < 2, velocity[1], velocity[0]) * 0.5
    inward = jnp.where(side % 2 == 0, normal, -normal) * 0.5
    half_z = velocity[2] * 0.5
    border = slice(0, TILE)
    inner = slice(TILE, 2 * TILE)
    for i in range(depth):
        warm = warmth(start[i + 2, 0:8, border], 1)
        store_rate(rate, slice(i * TILE, (i + 1) * TILE), start[i + 2, :, border], warm)
    source = sources(rate, mixed)
    totals = []
    for i in range(depth):
        cells = start[i + 2, :, border]
        gap = start[i + 2, :, inner] - cells
        behind = jnp.where(at_low, cells, pltpu.roll(cells, 1, 1))
        ahead = jnp.where(at_high, cells, pltpu.roll(cells, TILE - 1, 1))
        z_low = start[i + 1, :, border]
        z_high = start[i + 3, :, border]
        drift = inward * gap + along * (ahead - behind) + half_z * (z_high - z_low)
        spread = gap + (ahead + behind) + (z_high + z_low) - 4.0 * cells
        change = source[:, i * TILE : (i + 1) * TILE] - drift + diffuse * spread
        later = cells + time_step * change
        totals.append((normal * cells + normal * later) * 0.5)
    for k in range(layers):
        faces[:, k * TILE : (k + 1) * TILE] = totals[2 * k] + totals[2 * k + 1]
    summed = exact_dot(faces[...], place[...])
    out[:, 0, :] = summed[:fields] - fluxes[:, 0, :]


def vmem(count):
    return [pl.BlockSpec(memory_space=pltpu.VMEM)] * count


def smem(count):
    return [pl.BlockSpec(memory_space=pltpu.SMEM)] * count


def fine_step(velocity, patch_owner, stoich, diffusivity, blocks, slots, direct):
    fields = blocks[0].shape[1]
    layers = blocks[0].shape[2] // CELLS - 4
    rows = up(slots * fields, 8)
    pad = up(rows, 16)
    full, same = interpolation()
    weights = jnp.asarray(np.concatenate([full, same], 1), jnp.bfloat16)
    cells = 2 * layers * AREA
    out = pl.pallas_call(
        functools.partial(step_kernel, layers, slots, direct),
        in_specs=smem(2) + vmem(1) + smem(1) + vmem(1 + len(blocks)),
        out_specs=pl.BlockSpec(memory_space=pltpu.VMEM),
        out_shape=jax.ShapeDtypeStruct((fields, slots, cells), jnp.float32),
        scratch_shapes=[
            pltpu.VMEM((slots,) + blocks[0].shape[1:], jnp.bfloat16),
            pltpu.VMEM(((layers + 4) * pad, CELLS), jnp.bfloat16),
            pltpu.VMEM(((layers + 4) * pad, 2 * AREA), jnp.float32),
            pltpu.VMEM((2 * layers + 4, rows, AREA), jnp.float32),
            pltpu.VMEM((2 * layers + 2, rows, AREA), jnp.float32),
            pltpu.VMEM((3 * pad, AREA), jnp.bfloat16),
        ],
        cost_estimate=pl.CostEstimate(
            flops=4000000000, bytes_accessed=8000000, transcendentals=0
        ),
        name="fine_step",
    )(velocity, patch_owner, stoich, diffusivity, weights, *blocks)
    return out.transpose(1, 0, 2)


def side_fluxes(velocity, stoich, diffusivity, block, fluxes):
    fields = block.shape[1]
    layers = block.shape[2] // CELLS - 4
    rows = up(fields, 8)
    pad = up(rows, 16)
    full, same = interpolation()
    border, inner = strips()
    picked = np.concatenate([border, inner])
    weights = jnp.asarray(np.concatenate([full[:, picked], same[:, picked]], 1), jnp.bfloat16)
    place = jnp.asarray(pair_sums(layers))
    return pl.pallas_call(
        functools.partial(side_kernel, layers),
        in_specs=smem(1) + vmem(1) + smem(1) + vmem(4),
        out_specs=pl.BlockSpec(memory_space=pltpu.VMEM),
        out_shape=jax.ShapeDtypeStruct((fields, 1, fluxes.shape[2]), jnp.float32),
        scratch_shapes=[
            pltpu.VMEM(((layers + 4) * pad, CELLS), jnp.bfloat16),
            pltpu.VMEM(((layers + 4) * pad, 4 * TILE), jnp.float32),
            pltpu.VMEM((2 * layers + 4, rows, 2 * TILE), jnp.float32),
            pltpu.VMEM((3 * pad, 2 * layers * TILE), jnp.bfloat16),
            pltpu.VMEM((rows, layers * TILE), jnp.float32),
        ],
        cost_estimate=pl.CostEstimate(
            flops=800000000, bytes_accessed=2000000, transcendentals=0
        ),
        name="side_fluxes",
    )(velocity, stoich, diffusivity, weights, place, fluxes.transpose(1, 0, 2), block).transpose(
        1, 0, 2
    )


def with_halo(block):
    count = lax.axis_size("gy")
    forward = [(i, i + 1) for i in range(count - 1)]
    backward = [(i + 1, i) for i in range(count - 1)]
    low = lax.ppermute(block[:, :, -2 * CELLS :], "gy", forward)
    high = lax.ppermute(block[:, :, : 2 * CELLS], "gy", backward)
    return jnp.concatenate([low, block, high], 2)


def fetch(block, patch_owner, slots):
    groups = lax.axis_size("gx")
    if groups > DIRECT:
        my_slots = lax.axis_index("gx") * slots + jnp.arange(slots, dtype=jnp.int32)
        chooser = (my_slots[:, None] == patch_owner[None, :]).astype(block.dtype)
        everything = lax.all_gather(block, "gx", axis=0, tiled=True)
        return [jnp.einsum("oq,qfc->ofc", chooser, everything)], False
    blocks = [block] + [
        lax.ppermute(block, "gx", [(i, (i + shift) % groups) for i in range(groups)])
        for shift in range(1, groups)
    ]
    return blocks, True


def shards(coarse_send, coarse_flux, patch_owner, velocity, diffusivity, stoich):
    send_slots = coarse_send.shape[0]
    slots = 2 * send_slots
    block = with_halo(coarse_send)
    blocks, direct = fetch(block, patch_owner, slots)
    reflux = [
        side_fluxes(velocity, stoich, diffusivity, block[s : s + 1], coarse_flux[s : s + 1])
        for s in range(send_slots)
    ]
    fine_state = fine_step(velocity, patch_owner, stoich, diffusivity, blocks, slots, direct)
    return fine_state, jnp.concatenate(reflux, 0)


def solution(mesh):
    placed = (P("gx", None, "gy"), P("gx", None, "gy"), P(), P(), P(), P())
    return jax.shard_map(
        shards,
        mesh=mesh,
        in_specs=placed,
        out_specs=(P("gx", None, "gy"), P("gx", None, "gy")),
        check_vma=False,
    )
```

```python
import functools

import jax
import jax.numpy as jnp
import numpy as np
from jax import lax
from jax.experimental import pallas as pl
from jax.experimental.pallas import tpu as pltpu
from jax.sharding import PartitionSpec as P

CB = 16
FINE = 2 * CB
CELLS = CB * CB
AREA = FINE * FINE
TILE = 128
DIRECT = 8

time_step = 0.25
heat_gain = 2.0


def interpolation():
    slope = np.zeros((CB, CB), np.float32)
    for i in range(1, CB - 1):
        slope[i + 1, i], slope[i - 1, i] = 0.5, -0.5
    slope[1, 0], slope[0, 0] = 1.0, -1.0
    slope[-1, -1], slope[-2, -1] = 1.0, -1.0
    copy = np.zeros((CB, FINE), np.float32)
    tilt = np.zeros((CB, FINE), np.float32)
    for i in range(CB):
        for a in range(2):
            copy[i, 2 * i + a] = 1.0
            tilt[:, 2 * i + a] = slope[:, i] * (a - 0.5) * 0.5
    same = np.kron(copy, copy)
    full = same + np.kron(copy, tilt) + np.kron(tilt, copy)
    return full, same


def strips():
    edge = np.arange(FINE)
    last = FINE - 1
    border = [edge * FINE, edge * FINE + last, edge, last * FINE + edge]
    inner = [edge * FINE + 1, edge * FINE + last - 1, FINE + edge, (last - 1) * FINE + edge]
    return np.concatenate(border), np.concatenate(inner)


def pair_sums(layers):
    place = np.zeros((layers * TILE, layers * TILE // 2), np.float32)
    for k in range(layers):
        for lane in range(TILE):
            place[k * TILE + lane, k * TILE // 2 + lane // 2] = 0.25
    return place


def up(value, unit):
    return -(-value // unit) * unit


def equal(shape, left, right):
    rows = lax.broadcasted_iota(jnp.int32, shape, 0)
    columns = lax.broadcasted_iota(jnp.int32, shape, 1)
    return left(rows) == right(columns)


def fill_coarse(stack, blocks, rows, layers):
    slots = len(blocks)
    fields = blocks[0].shape[0]
    mixed = None
    for s in range(slots):
        spot = equal((rows, fields), lambda r: r, lambda f: f * slots + s)
        part = jnp.dot(
            spot.astype(jnp.float32).astype(jnp.bfloat16),
            blocks[s],
            preferred_element_type=jnp.float32,
        )
        mixed = part if mixed is None else mixed + part
    pad = up(rows, 16)
    for k in range(layers + 4):
        stack[k * pad : k * pad + rows, :] = mixed[:, k * CELLS : (k + 1) * CELLS].astype(
            jnp.bfloat16
        )


def edge_ghosts(parts, bottom, top, layers, width, count):
    pad = up(count, 16)

    def rows(k):
        return slice((k + 2) * pad, (k + 2) * pad + count)

    @pl.when(bottom)
    def _():
        parts[rows(-1), width:] = 2.0 * parts[rows(0), width:] - parts[rows(1), width:]

    @pl.when(top)
    def _():
        parts[rows(layers), width:] = (
            2.0 * parts[rows(layers - 1), width:] - parts[rows(layers - 2), width:]
        )


def fine_layers(start, parts, layers, width, count):
    step = 2 * TILE
    pad = up(count, 16)

    def rows(k):
        return pl.ds(pl.multiple_of((k + 1) * pad, 16), count)

    def body(k, carry):
        for c in range(0, width, step):
            lanes = slice(c, c + step)
            copies = slice(width + c, width + c + step)
            centre = parts[rows(k), lanes]
            tilt = (parts[rows(k + 1), copies] - parts[rows(k - 1), copies]) * 0.125
            start[2 * k, :, lanes] = centre - tilt
            start[2 * k + 1, :, lanes] = centre + tilt
        return carry

    lax.fori_loop(0, layers + 2, body, 0)


def exact_dot(left, right):
    return jnp.dot(
        left, right, precision=lax.Precision.HIGHEST, preferred_element_type=jnp.float32
    )


def split_coupling(stoich, slots, rows):
    value = stoich[...]
    fields = value.shape[0]
    pad = up(rows, 16)
    width = 3 * pad
    rise = equal((rows, fields), lambda r: r // slots, lambda f: f).astype(jnp.float32)
    run = equal((fields, width), lambda f: f, lambda c: c % pad // slots).astype(jnp.float32)
    spread = exact_dot(rise, exact_dot(value, run))
    shape = (rows, width)
    spread = jnp.where(equal(shape, lambda r: r % slots, lambda c: c % pad % slots), spread, 0.0)
    head = spread.astype(jnp.bfloat16)
    rest = (spread - head.astype(jnp.float32)).astype(jnp.bfloat16)
    column = lax.broadcasted_iota(jnp.int32, shape, 1)
    return jnp.where(
        column < 2 * pad, head.astype(jnp.float32), rest.astype(jnp.float32)
    ).astype(jnp.bfloat16)


def spread_diffusivity(diffusivity, slots, rows):
    field = lax.broadcasted_iota(jnp.int32, (rows, TILE), 0) // slots
    value = jnp.zeros((rows, TILE), jnp.float32)
    for f in range(diffusivity.shape[0]):
        value = jnp.where(field == f, diffusivity[f], value)
    return value


def warmth(field, slots):
    warm = jax.nn.sigmoid(heat_gain * field[0:slots])
    row = lax.broadcasted_iota(jnp.int32, (8, field.shape[1]), 0) % slots
    value = jnp.broadcast_to(warm[0:1], row.shape)
    for s in range(1, slots):
        value = jnp.where(row == s, warm[s : s + 1], value)
    return value


def store_rate(rate, lanes, cells, warm):
    rows = cells.shape[0]
    pad = up(rows, 16)
    value = cells * jnp.concatenate([warm] * (rows // 8), 0)
    head = value.astype(jnp.bfloat16)
    rest = (value - head.astype(jnp.float32)).astype(jnp.bfloat16)
    rate[0:rows, lanes] = head
    rate[pad : pad + rows, lanes] = rest
    rate[2 * pad : 2 * pad + rows, lanes] = head


def sources(rate, mixed):
    return jnp.dot(mixed, rate[...], preferred_element_type=jnp.float32)


def stage(field, z, slots, rate, mixed, velocity, diffuse, emit):
    count = AREA // TILE
    lane = lax.broadcasted_iota(jnp.int32, diffuse.shape, 1)
    pos = lane % FINE
    at_low, at_high = pos == 0, pos == FINE - 1
    head, tail = lane < FINE, lane >= TILE - FINE
    half = [velocity[d] * 0.5 for d in range(3)]
    warm = warmth(field[z, 0:8, :], slots)
    for t in range(count):
        lanes = slice(t * TILE, (t + 1) * TILE)
        store_rate(rate, lanes, field[z, :, lanes], warm[:, lanes])
    source = sources(rate, mixed)
    tiles = {}
    ups = {}
    downs = {}

    def tile(t):
        if t not in tiles:
            tiles[t] = field[z, :, t * TILE : (t + 1) * TILE]
            ups[t] = pltpu.roll(tiles[t], TILE - FINE, 1)
            downs[t] = pltpu.roll(tiles[t], FINE, 1)
        return tiles[t]

    for t in range(count):
        lanes = slice(t * TILE, (t + 1) * TILE)
        cells = tile(t)
        x_low = jnp.where(at_low, cells, pltpu.roll(cells, 1, 1))
        x_high = jnp.where(at_high, cells, pltpu.roll(cells, TILE - 1, 1))
        if t + 1 < count:
            tile(t + 1)
        y_low = jnp.where(head, downs[t - 1] if t else cells, downs[t])
        y_high = jnp.where(tail, ups[t + 1] if t + 1 < count else cells, ups[t])
        z_low = field[z - 1, :, lanes]
        z_high = field[z + 1, :, lanes]
        drift = (
            half[0] * (x_high - x_low) + half[1] * (y_high - y_low) + half[2] * (z_high - z_low)
        )
        spread = (x_high + x_low) + (y_high + y_low) + (z_high + z_low) - 6.0 * cells
        emit(lanes, cells, source[:, lanes] - drift + diffuse * spread)


def join(picked, low, centres, high):
    edge = 2 * CELLS
    cells = centres[0].shape[2]
    for s in range(picked.shape[0]):
        picked[s, :, :edge] = low[s]
        middle = centres[0][s]
        for other in centres[1:]:
            middle = middle + other[s]
        picked[s, :, edge : edge + cells] = middle
        picked[s, :, edge + cells :] = high[s]


def pick_kernel(slots, owner, *refs):
    blocks = refs[:-2]
    mine, theirs = refs[-2:]
    groups = lax.axis_size("gx")
    group = lax.axis_index("gx")
    partner = group + 1 - 2 * lax.rem(group, 2)
    mine[...] = jnp.zeros_like(mine)
    theirs[...] = jnp.zeros_like(theirs)
    for j, block in enumerate(blocks):
        origin = lax.rem(group - 2 * j + groups, groups)
        for t in range(block.shape[0]):
            slot = owner[origin * block.shape[0] + t]
            for s in range(slots):

                @pl.when(slot == group * slots + s)
                def _():
                    mine[s] = block[t]

                @pl.when(slot == partner * slots + s)
                def _():
                    theirs[s] = block[t]


def step_kernel(layers, slots, velocity, stoich, diffusivity, weights, *refs):
    low, high, *centres = refs[:-7]
    out, picked, stack, parts, start, middle, rate = refs[-7:]
    pencil = lax.axis_index("gy")
    bottom, top = pencil == 0, pencil == lax.axis_size("gy") - 1
    depth = 2 * layers
    rows = start.shape[1]
    rate[...] = jnp.zeros_like(rate)
    join(picked, low, centres, high)
    fill_coarse(stack, [picked[s] for s in range(slots)], rows, layers)
    parts[...] = jnp.dot(stack[...], weights[...], preferred_element_type=jnp.float32)
    edge_ghosts(parts, bottom, top, layers, AREA, rows)
    fine_layers(start, parts, layers, AREA, rows)

    @pl.when(bottom)
    def _():
        start[1] = start[2]

    @pl.when(top)
    def _():
        start[depth + 2] = start[depth + 1]

    mixed = split_coupling(stoich, slots, rows)
    diffuse = spread_diffusivity(diffusivity, slots, rows)

    def first(i, carry):
        def emit(lanes, cells, change):
            middle[i, :, lanes] = cells + time_step * change

        stage(start, i + 1, slots, rate, mixed, velocity, diffuse, emit)
        return carry

    lax.fori_loop(0, depth + 2, first, 0)

    @pl.when(bottom)
    def _():
        middle[0] = middle[1]

    @pl.when(top)
    def _():
        middle[depth + 1] = middle[depth]

    def second(i, carry):
        def emit(lanes, cells, change):
            value = (start[i + 2, :, lanes] + cells) * 0.5 + (time_step * 0.5) * change
            at = pl.multiple_of(i * AREA + lanes.start, TILE)
            for f in range(out.shape[0]):
                out[f, :, pl.ds(at, TILE)] = value[f * slots : (f + 1) * slots]

        stage(middle, i + 1, slots, rate, mixed, velocity, diffuse, emit)
        return carry

    lax.fori_loop(0, depth, second, 0)


def side_kernel(
    layers, velocity, stoich, diffusivity, weights, place, fluxes, low, high, own, out, picked,
    stack, parts, start, rate, faces,
):
    pencil = lax.axis_index("gy")
    bottom, top = pencil == 0, pencil == lax.axis_size("gy") - 1
    fields = own.shape[1]
    depth = 2 * layers
    width = 2 * TILE
    rows = start.shape[1]
    rate[...] = jnp.zeros_like(rate)
    join(picked, low, [own], high)
    fill_coarse(stack, [picked[0]], rows, layers)
    parts[...] = jnp.dot(stack[...], weights[...], preferred_element_type=jnp.float32)
    edge_ghosts(parts, bottom, top, layers, width, rows)
    fine_layers(start, parts, layers, width, rows)

    @pl.when(bottom)
    def _():
        start[1] = start[2]

    @pl.when(top)
    def _():
        start[depth + 2] = start[depth + 1]

    mixed = split_coupling(stoich, 1, rows)
    diffuse = spread_diffusivity(diffusivity, 1, rows)
    lane = lax.broadcasted_iota(jnp.int32, (rows, TILE), 1)
    pos = lane % FINE
    side = lane // FINE
    at_low, at_high = pos == 0, pos == FINE - 1
    normal = jnp.where(side < 2, velocity[0], velocity[1])
    along = jnp.where(side < 2, velocity[1], velocity[0]) * 0.5
    inward = jnp.where(side % 2 == 0, normal, -normal) * 0.5
    half_z = velocity[2] * 0.5
    border = slice(0, TILE)
    inner = slice(TILE, 2 * TILE)
    for i in range(depth):
        warm = warmth(start[i + 2, 0:8, border], 1)
        store_rate(rate, slice(i * TILE, (i + 1) * TILE), start[i + 2, :, border], warm)
    source = sources(rate, mixed)
    totals = []
    for i in range(depth):
        cells = start[i + 2, :, border]
        gap = start[i + 2, :, inner] - cells
        behind = jnp.where(at_low, cells, pltpu.roll(cells, 1, 1))
        ahead = jnp.where(at_high, cells, pltpu.roll(cells, TILE - 1, 1))
        z_low = start[i + 1, :, border]
        z_high = start[i + 3, :, border]
        drift = inward * gap + along * (ahead - behind) + half_z * (z_high - z_low)
        spread = gap + (ahead + behind) + (z_high + z_low) - 4.0 * cells
        change = source[:, i * TILE : (i + 1) * TILE] - drift + diffuse * spread
        later = cells + time_step * change
        totals.append((normal * cells + normal * later) * 0.5)
    for k in range(layers):
        faces[:, k * TILE : (k + 1) * TILE] = totals[2 * k] + totals[2 * k + 1]
    summed = exact_dot(faces[...], place[...])
    out[:, 0, :] = summed[:fields] - fluxes[:, 0, :]


def vmem(count):
    return [pl.BlockSpec(memory_space=pltpu.VMEM)] * count


def smem(count):
    return [pl.BlockSpec(memory_space=pltpu.SMEM)] * count


def fine_step(velocity, stoich, diffusivity, low, high, centres):
    slots, fields, cells = centres[0].shape
    layers = cells // CELLS
    rows = up(slots * fields, 8)
    pad = up(rows, 16)
    full, same = interpolation()
    weights = jnp.asarray(np.concatenate([full, same], 1), jnp.bfloat16)
    cells = 2 * layers * AREA
    out = pl.pallas_call(
        functools.partial(step_kernel, layers, slots),
        in_specs=smem(1) + vmem(1) + smem(1) + vmem(3 + len(centres)),
        out_specs=pl.BlockSpec(memory_space=pltpu.VMEM),
        out_shape=jax.ShapeDtypeStruct((fields, slots, cells), jnp.float32),
        scratch_shapes=[
            pltpu.VMEM((slots, fields, (layers + 4) * CELLS), jnp.bfloat16),
            pltpu.VMEM(((layers + 4) * pad, CELLS), jnp.bfloat16),
            pltpu.VMEM(((layers + 4) * pad, 2 * AREA), jnp.float32),
            pltpu.VMEM((2 * layers + 4, rows, AREA), jnp.float32),
            pltpu.VMEM((2 * layers + 2, rows, AREA), jnp.float32),
            pltpu.VMEM((3 * pad, AREA), jnp.bfloat16),
        ],
        cost_estimate=pl.CostEstimate(
            flops=4000000000, bytes_accessed=8000000, transcendentals=0
        ),
        name="fine_step",
    )(velocity, stoich, diffusivity, weights, low, high, *centres)
    return out.transpose(1, 0, 2)


def side_fluxes(velocity, stoich, diffusivity, low, high, own, fluxes):
    fields = own.shape[1]
    layers = own.shape[2] // CELLS
    rows = up(fields, 8)
    pad = up(rows, 16)
    full, same = interpolation()
    border, inner = strips()
    picked = np.concatenate([border, inner])
    weights = jnp.asarray(np.concatenate([full[:, picked], same[:, picked]], 1), jnp.bfloat16)
    place = jnp.asarray(pair_sums(layers))
    return pl.pallas_call(
        functools.partial(side_kernel, layers),
        in_specs=smem(1) + vmem(1) + smem(1) + vmem(6),
        out_specs=pl.BlockSpec(memory_space=pltpu.VMEM),
        out_shape=jax.ShapeDtypeStruct((fields, 1, fluxes.shape[2]), jnp.float32),
        scratch_shapes=[
            pltpu.VMEM((1, fields, (layers + 4) * CELLS), jnp.bfloat16),
            pltpu.VMEM(((layers + 4) * pad, CELLS), jnp.bfloat16),
            pltpu.VMEM(((layers + 4) * pad, 4 * TILE), jnp.float32),
            pltpu.VMEM((2 * layers + 4, rows, 2 * TILE), jnp.float32),
            pltpu.VMEM((3 * pad, 2 * layers * TILE), jnp.bfloat16),
            pltpu.VMEM((rows, layers * TILE), jnp.float32),
        ],
        cost_estimate=pl.CostEstimate(
            flops=800000000, bytes_accessed=2000000, transcendentals=0
        ),
        name="side_fluxes",
    )(
        velocity, stoich, diffusivity, weights, place, fluxes.transpose(1, 0, 2), low, high, own
    ).transpose(1, 0, 2)


def halo(blocks):
    count = lax.axis_size("gy")
    forward = [(i, i + 1) for i in range(count - 1)]
    backward = [(i + 1, i) for i in range(count - 1)]
    last = sum(block[:, :, -2 * CELLS :] for block in blocks)
    first = sum(block[:, :, : 2 * CELLS] for block in blocks)
    return lax.ppermute(last, "gy", forward), lax.ppermute(first, "gy", backward)


def fetch(own, patch_owner, slots):
    groups = lax.axis_size("gx")
    if groups > DIRECT or groups % 2:
        my_slots = lax.axis_index("gx") * slots + jnp.arange(slots, dtype=jnp.int32)
        chooser = (my_slots[:, None] == patch_owner[None, :]).astype(own.dtype)
        everything = lax.all_gather(own, "gx", axis=0, tiled=True)
        return [jnp.einsum("oq,qfc->ofc", chooser, everything)]
    blocks = [own] + [
        lax.ppermute(own, "gx", [(i, (i + shift) % groups) for i in range(groups)])
        for shift in range(2, groups, 2)
    ]
    shape = jax.ShapeDtypeStruct((slots,) + own.shape[1:], own.dtype)
    mine, theirs = pl.pallas_call(
        functools.partial(pick_kernel, slots),
        in_specs=smem(1) + vmem(len(blocks)),
        out_specs=vmem(2),
        out_shape=[shape, shape],
        cost_estimate=pl.CostEstimate(
            flops=200000000, bytes_accessed=1000000, transcendentals=0
        ),
        name="pick",
    )(patch_owner, *blocks)
    return [mine, lax.ppermute(theirs, "gx", [(i, i ^ 1) for i in range(groups)])]


def shards(coarse_send, coarse_flux, patch_owner, velocity, diffusivity, stoich):
    send_slots = coarse_send.shape[0]
    centres = fetch(coarse_send, patch_owner, 2 * send_slots)
    low, high = halo([coarse_send])
    reflux = [
        side_fluxes(
            velocity, stoich, diffusivity, *(a[s : s + 1] for a in (low, high, coarse_send, coarse_flux))
        )
        for s in range(send_slots)
    ]
    fine_state = fine_step(velocity, stoich, diffusivity, *halo(centres), centres)
    return fine_state, jnp.concatenate(reflux, 0)


def solution(mesh):
    placed = (P("gx", None, "gy"), P("gx", None, "gy"), P(), P(), P(), P())
    return jax.shard_map(
        shards,
        mesh=mesh,
        in_specs=placed,
        out_specs=(P("gx", None, "gy"), P("gx", None, "gy")),
        check_vma=False,
    )
```
